32 devices in a mesh: groups: 2 (over y), shot: 4 (over x, core), slab: 4 (over z).
Axes of the slice: x: 2, y: 2, z: 4, core: 2. Of those that a mesh axis runs over, the one named last changes fastest.
Arguments:
- slowness: float32 [32, 192, 128], P(('groups', 'slab')), parts along dimension 0, may hold values from 0.8 to 1.25
- wave_prev: float32 [8, 16, 192, 128], P(('groups', 'shot'), 'slab'), parts along dimension 0, may hold values from -6 to 6
- wave_now: float32 [8, 16, 192, 128], P(('groups', 'shot'), 'slab'), parts along dimension 0, may hold values from -6 to 6
- memory: float32 [8, 3, 16, 192, 128], P(('groups', 'shot'), None, 'slab'), parts along dimension 0, may hold values from -6 to 6
- adjoint_now: float32 [8, 16, 192, 128], P(('groups', 'shot'), 'slab'), parts along dimension 0, may hold values from -6 to 6
- adjoint_prev: float32 [8, 16, 192, 128], P(('groups', 'shot'), 'slab'), parts along dimension 0, may hold values from -6 to 6
- wavelet: float32 [4], replicated, may hold values from -16 to 16
- src_cells: int32 [8, 64], P(('groups', 'shot')), parts along dimension 0, may hold values from 0 to 393215
- src_signs: int32 [8, 64], P(('groups', 'shot')), parts along dimension 0, may hold values from -1 to 1, as said below
- rec_cells: int32 [512], P('groups'), parts along dimension 0, may hold values from 0 to 393215
- observed: float32 [8, 4, 256], P(('groups', 'shot')), parts along dimension 0, may hold values from -6 to 6
Outputs:
- new_slowness: float32 [32, 192, 128], P(('groups', 'slab')), parts along dimension 0
- gradient: float32 [32, 192, 128], P(('groups', 'slab'), 'shot'), parts along dimension 0
The draws below stay inside these ranges and needn't reach their ends.
There are 2 independent parts, one for each index of `groups`. The reference program is written for one: setup_inputs(seed, part) draws one part's arguments, and reference() takes and returns one part's arrays. A program takes and returns all parts, laid end to end along the dimension named above; an argument that names none is the same for every part. Nothing has to cross between parts.
Inputs may be any that keep to these rules, and one draw needn't show every extreme that they name: `src_signs`: each entry is -1 or +1.
All inputs are finite; a program needn't handle non-finite values.
Results may differ from the reference program's by a relative error of at most 0.0001.
Values sent between devices are 32-bit elements; how exact they have to be, the bound alone decides.
No kernel may reach another device: no remote copies, remote signals or barrier semaphores. Data moves between devices by JAX's collectives and lax.ppermute only.
A program may use at most 64 MiB of HBM per device.

```python
import jax
import jax.numpy as jnp
from jax import lax

NX = 192
NY = 128
STEPS = 4
NMECH = 3
NSRC = 64
NREC = 256
SHOTS = 4
NZ = 16


def draw_src_signs(key, part):
    picked = jax.random.randint(key, (SHOTS, NSRC), 0, 2)
    signs = 2 * picked - 1
    signs = signs.at[:, 0].set(1).at[:, 1].set(-1)
    return signs.astype(jnp.int32)


def set_ends(values, stream_key, low, high):
    index_at = [jax.random.randint(jax.random.fold_in(stream_key, axis), (), 0, length) for axis, length in enumerate(values.shape)]
    longest = values.shape.index(max(values.shape))
    beside = index_at[:longest] + [(index_at[longest] + 1) % values.shape[longest]] + index_at[longest + 1:]
    return values.at[tuple(index_at)].set(low).at[tuple(beside)].set(high)


def shard_levels(stream_key, extent, shards, least, top_value):
    gain, own = 1.0, jax.random.fold_in(stream_key, 6)
    for position, shards_of in shards:
        heights = jnp.exp(jax.random.uniform(jax.random.fold_in(own, position), (shards_of,), jnp.float32, least / len(shards), top_value / len(shards)))
        gain = gain * jnp.repeat(heights, extent[position] // shards_of).reshape([-1 if axis == position else 1 for axis in range(len(extent))])
    return gain


def gaussian(own_key, dims, spread, most, split=(), held_as=jnp.bfloat16):
    level = shard_levels(own_key, dims, split, -0.22, 0.18) if split else 1.0
    result = jax.random.normal(own_key, dims, jnp.float32) * spread * level
    return jnp.minimum(jnp.maximum(result, -most), most).astype(held_as)


def setup_inputs(seed: int = 0, part: int = 0) -> dict:
    keys = jax.random.split(jax.random.key(seed), 12)
    part_keys = jax.random.split(jax.random.fold_in(keys[11], part), 12)
    return {
        "slowness": jnp.clip(0.8 + 0.45 * jax.random.uniform(part_keys[0], (NZ, NX, NY), jnp.float32) ** shard_levels(part_keys[0], (NZ, NX, NY), ((0, 4),), -0.2, 0.2), 0.8, 1.25),
        "wave_prev": gaussian(part_keys[1], (SHOTS, NZ, NX, NY), 1.0, 6.0, ((0, 4), (1, 4)), jnp.float32),
        "wave_now": gaussian(part_keys[2], (SHOTS, NZ, NX, NY), 1.0, 6.0, ((0, 4), (1, 4)), jnp.float32),
        "memory": gaussian(part_keys[3], (SHOTS, NMECH, NZ, NX, NY), 1.0, 6.0, ((0, 4), (2, 4)), jnp.float32),
        "adjoint_now": gaussian(part_keys[4], (SHOTS, NZ, NX, NY), 1.0, 6.0, ((0, 4), (1, 4)), jnp.float32),
        "adjoint_prev": gaussian(part_keys[5], (SHOTS, NZ, NX, NY), 1.0, 6.0, ((0, 4), (1, 4)), jnp.float32),
        "wavelet": gaussian(keys[6], (STEPS,), 4.0, 16.0, (), jnp.float32),
        "src_cells": set_ends(jax.random.randint(part_keys[7], (SHOTS, NSRC), 0, NZ * NX * NY), jax.random.fold_in(part_keys[7], 1), 0, (NZ * NX * NY) - 1).astype(jnp.int32),
        "src_signs": draw_src_signs(jax.random.fold_in(jax.random.fold_in(keys[11], part), 71), part),
        "rec_cells": set_ends(jax.random.randint(part_keys[9], (NREC,), 0, NZ * NX * NY), jax.random.fold_in(part_keys[9], 1), 0, (NZ * NX * NY) - 1).astype(jnp.int32),
        "observed": gaussian(part_keys[10], (SHOTS, STEPS, NREC), 1.0, 6.0, ((0, 4),), jnp.float32),
    }


center_coef = -2.5
near_coef = 4.0 / 3.0
far_coef = -1.0 / 12.0
courant = 0.14
relax_decay = (0.3, 0.7, 0.95)
relax_weight = (0.3, 0.2, 0.1)
update_rate = 0.05
tiny_eps = 1e-06

def laplace(padded):
    middle = padded[2:-2]
    flanks = jnp.pad(middle, ((0, 0), (2, 2), (2, 2)))
    depth_sum = near_coef * (padded[3:-1] + padded[1:-3]) + far_coef * (padded[4:] + padded[:-4])
    cross_sum = near_coef * (flanks[:, 3:-1, 2:-2] + flanks[:, 1:-3, 2:-2]) + far_coef * (flanks[:, 4:, 2:-2] + flanks[:, :-4, 2:-2])
    along_sum = near_coef * (flanks[:, 2:-2, 3:-1] + flanks[:, 2:-2, 1:-3]) + far_coef * (flanks[:, 2:-2, 4:] + flanks[:, 2:-2, :-4])
    return 3.0 * center_coef * middle + depth_sum + cross_sum + along_sum

def forward_shot(slowness, older, current, relax, src_field, wavelet, rec_cells):
    decay = jnp.array(relax_decay, jnp.float32)[:, None, None, None]
    weight = jnp.array(relax_weight, jnp.float32)[:, None, None, None]
    scaled = courant / (slowness * slowness)
    traces = []
    for level in range(STEPS):
        curved = laplace(jnp.pad(current, ((2, 2), (0, 0), (0, 0))))
        accel = curved + lax.optimization_barrier(jnp.sum(relax, 0))
        newer = 2.0 * current - older + scaled * accel + wavelet[level] * src_field
        relax = decay * relax - weight * curved[None]
        older, current = (current, newer)
        traces.append(current.reshape(-1)[rec_cells])
    return (jnp.stack(traces), current, older)

def reference(slowness, wave_prev, wave_now, memory, adjoint_now, adjoint_prev, wavelet, src_cells, src_signs, rec_cells, observed):

    def per_shot(total, items):
        older, current, relax, back_now, back_prev, cells, signs, seen = items
        src_field = jnp.zeros((NZ * NX * NY,), jnp.float32).at[cells].add(signs.astype(jnp.float32)).reshape(NZ, NX, NY)

        def model_map(model):
            return forward_shot(model, older, current, relax, src_field, wavelet, rec_cells)
        outputs, pullback = jax.vjp(model_map, slowness)
        grad_s, = pullback((outputs[0] - seen, back_now, back_prev))
        return (total + grad_s, None)
    start = jnp.zeros((NZ, NX, NY), jnp.float32)
    total, _ = lax.scan(per_shot, start, (wave_prev, wave_now, memory, adjoint_now, adjoint_prev, src_cells, src_signs, observed))
    squares = jnp.sum(total * total)
    rms_value = jnp.sqrt(squares / (NZ * NX * NY) + tiny_eps)
    gradient = total / rms_value
    new_slowness = slowness - update_rate * gradient
    return (new_slowness, gradient)
```

```python
import jax
import jax.numpy as jnp
from jax import lax
from jax.experimental import pallas as pl
from jax.experimental.pallas import tpu as pltpu
from jax.sharding import PartitionSpec as P

STEPS = 4

center_coef = -2.5
near_coef = 4.0 / 3.0
far_coef = -1.0 / 12.0
courant = 0.14
relax_decay = (0.3, 0.7, 0.95)
relax_weight = (0.3, 0.2, 0.1)
update_rate = 0.05
tiny_eps = 1e-06

echo = tuple(
    sum(b * a**k for a, b in zip(relax_decay, relax_weight)) for k in range(STEPS)
)

PAD = 8
VMEM_SPEC = pl.BlockSpec(memory_space=pltpu.VMEM)
SMEM_SPEC = pl.BlockSpec(memory_space=pltpu.SMEM)
F32 = jnp.float32


def run(kernel, name, outs, args, scratch=(), smem=(), cost=200_000):
    specs = [SMEM_SPEC if i in smem else VMEM_SPEC for i in range(len(args))]
    return pl.pallas_call(
        kernel,
        name=name,
        out_shape=[jax.ShapeDtypeStruct(shape, F32) for shape in outs],
        in_specs=specs,
        out_specs=[VMEM_SPEC] * len(outs),
        scratch_shapes=list(scratch),
        compiler_params=pltpu.CompilerParams(vmem_limit_bytes=12 << 20),
        cost_estimate=pl.CostEstimate(flops=cost, bytes_accessed=cost, transcendentals=0),
    )(*args)


def chunks(width):
    step = 64 if width % 64 == 0 else 8
    return [(start, step) for start in range(0, width, step)]


def clear_pads(pad):
    depth, tall, lanes = pad.shape
    for p in range(depth):
        pad[p, :PAD] = jnp.zeros((PAD, lanes), F32)
        pad[p, tall - PAD :] = jnp.zeros((PAD, lanes), F32)


def own_laplace(pad, p, r, n):
    depth, _, lanes = pad.shape

    def at(plane, shift):
        return pad[plane, PAD + r + shift : PAD + r + shift + n]

    middle = at(p, 0)
    near = at(p, 1) + at(p, -1)
    far = at(p, 2) + at(p, -2)
    for plane in (p - 1, p + 1):
        if 0 <= plane < depth:
            near += at(plane, 0)
    for plane in (p - 2, p + 2):
        if 0 <= plane < depth:
            far += at(plane, 0)
    lane = lax.broadcasted_iota(jnp.int32, (n, lanes), 1)
    near += jnp.where(lane >= 1, pltpu.roll(middle, 1, 1), 0.0)
    near += jnp.where(lane < lanes - 1, pltpu.roll(middle, lanes - 1, 1), 0.0)
    far += jnp.where(lane >= 2, pltpu.roll(middle, 2, 1), 0.0)
    far += jnp.where(lane < lanes - 2, pltpu.roll(middle, lanes - 2, 1), 0.0)
    return 3.0 * center_coef * middle + near_coef * near + far_coef * far


def ghosts(a, b, r, n):
    slab, count = lax.axis_index("slab"), lax.axis_size("slab")
    even = lax.rem(slab, 2) == 0
    low, high = [], []
    for j in range(2):
        from_a, from_b = a[j, r : r + n], b[j, r : r + n]
        zero = jnp.zeros_like(from_a)
        low.append(jnp.where(slab == 0, zero, jnp.where(even, from_b, from_a)))
        high.append(jnp.where(slab == count - 1, zero, jnp.where(even, from_a, from_b)))
    return low, high


def reach(low, high, p, depth):
    terms = []
    for distance, coef in ((1, near_coef), (2, far_coef)):
        below, above = p - distance, p + distance
        if below < 0:
            terms.append(coef * low[2 + below])
        if above >= depth:
            terms.append(coef * high[above - depth])
    return sum(terms[1:], terms[0]) if terms else 0.0


def complete(low, high, scale_low, scale_high, field, r, n):
    depth = field.shape[0]

    def row(p):
        return field[p, r : r + n]

    low = [
        low[0] + scale_low[0, r : r + n] * (far_coef * row(0)),
        low[1] + scale_low[1, r : r + n] * (near_coef * row(0) + far_coef * row(1)),
    ]
    high = [
        high[0]
        + scale_high[0, r : r + n] * (near_coef * row(depth - 1) + far_coef * row(depth - 2)),
        high[1] + scale_high[1, r : r + n] * (far_coef * row(depth - 1)),
    ]
    return low, high


def send_planes(a, b, field):
    depth = field.shape[0]
    odd = lax.rem(lax.axis_index("slab"), 2)
    top = depth - 2
    for j in range(2):
        a[j] = field[top * (1 - odd) + j]
        b[j] = field[top * odd + j]


def one_hot_rows(cells, first_row, rows, lanes):
    shift = lanes.bit_length() - 1
    row = lax.shift_right_arithmetic(cells, shift) - first_row
    at = lax.broadcasted_iota(jnp.int32, (rows, cells.shape[1]), 0)
    return jnp.where(at == row, 1.0, 0.0).astype(jnp.bfloat16)


def is_lane(cells, lanes):
    at = lax.broadcasted_iota(jnp.int32, (lanes, cells.shape[1]), 0)
    return at == jnp.bitwise_and(cells, lanes - 1)


def spread(rows, columns):
    return lax.dot_general(
        rows, columns, (((1,), (1,)), ((), ())), preferred_element_type=F32
    )


def per_device(
    slowness,
    wave_prev,
    wave_now,
    memory,
    adjoint_now,
    adjoint_prev,
    wavelet,
    src_cells,
    src_signs,
    rec_cells,
    observed,
):
    depth, width, lanes = slowness.shape
    slabs, shots = lax.axis_size("slab"), lax.axis_size("shot")
    mechanisms = memory.shape[1]
    assert depth >= 4 and depth % 2 == 0 and lanes & (lanes - 1) == 0
    assert slabs & (slabs - 1) == 0 and shots & (shots - 1) == 0 and shots > 1 and slabs > 1
    whole, pair, half = (depth, width, lanes), (2, width, lanes), (depth // 2, width, lanes)
    rows = chunks(width)
    planes = range(depth)
    padded = pltpu.VMEM((depth, width + 2 * PAD, lanes), F32)
    older, now, relax = wave_prev[0], wave_now[0], memory[0]
    back_now, back_prev = adjoint_now[0], adjoint_prev[0]
    receivers = rec_cells.reshape(1, -1)
    seen = observed[0]

    pairs_a = [(i, i ^ 1) for i in range(slabs)]
    pairs_b = []
    for s in range(shots):
        for k in range(slabs):
            mate = k + 1 if k % 2 else k - 1
            if 0 <= mate < slabs:
                pairs_b.append((s * slabs + k, s * slabs + mate))
            else:
                pairs_b.append((s * slabs + k, (s ^ 1) * slabs + k))

    def exchange(sends):
        return lax.ppermute(sends[0], "slab", pairs_a), lax.ppermute(
            sends[1], ("shot", "slab"), pairs_b
        )

    def shot_swap(value, bit):
        return lax.ppermute(value, "shot", [(i, i ^ bit) for i in range(shots)])

    def slab_swap(value, bit):
        return lax.ppermute(value, "slab", [(i, i ^ bit) for i in range(slabs)])

    def first_sends(field, model, a, b):
        send_planes(a, b, field)
        odd = lax.rem(lax.axis_index("slab"), 2)
        mine = lax.rem(lax.axis_index("shot"), 2)
        top = depth - 2
        a[2] = model[top * (1 - odd) + mine]
        b[2] = model[top * odd + mine]

    got_now = exchange(run(first_sends, "sends0", [(3, width, lanes)] * 2, (now, slowness)))

    def step0(field, before, variables, model, cells, signs, pulse, *outs):
        lap, newer, scaled, factor, source, rest0, rest1, rest2, rest3, a, b, pad = outs
        rests = (rest0, rest1, rest2, rest3)
        clear_pads(pad)
        for p in planes:
            pad[p, PAD : PAD + width] = field[p]
        first_row = lax.axis_index("slab") * (depth * width)
        columns = jnp.where(is_lane(cells[...], lanes), signs[...].astype(F32), 0.0)
        columns = columns.astype(jnp.bfloat16)
        for p in planes:
            source[p] = spread(
                one_hot_rows(cells[...], first_row + p * width, width, lanes), columns
            )
        for p in planes:
            for r, n in rows:
                at = (p, slice(r, r + n))
                inverse = 1.0 / model[at]
                scale = courant * (inverse * inverse)
                scaled[at] = scale
                factor[at] = -2.0 * (scale * inverse)
                parts = [variables[(l, *at)] for l in range(mechanisms)]
                for n_step in range(STEPS):
                    terms = [
                        part if n_step == 0 else a_l**n_step * part
                        for part, a_l in zip(parts, relax_decay)
                    ]
                    rests[n_step][at] = sum(terms[1:], terms[0])
                curved = own_laplace(pad, p, r, n)
                lap[at] = curved
                newer[at] = (
                    2.0 * field[at]
                    - before[at]
                    + scale * (curved + rests[0][at])
                    + pulse[0] * source[at]
                )
        send_planes(a, b, newer)

    lap0s, p1s, scaled, factor, source, rest0, rest1, rest2, rest3, *sends = run(
        step0,
        "step0",
        [whole] * 9 + [pair] * 2,
        (now, older, relax, slowness, src_cells, src_signs, wavelet),
        [padded],
        smem=(6,),
    )
    got_p1 = exchange(sends)

    def receive(cells, values, *outs):
        first_row = lax.axis_index("slab") * (depth * width)
        lane = is_lane(cells[...], lanes)
        columns = [jnp.where(lane, 1.0, 0.0).astype(jnp.bfloat16)]
        for level in range(STEPS):
            left = values[level : level + 1, :]
            for _ in range(3):
                piece = left.astype(jnp.bfloat16)
                columns.append(jnp.where(lane, piece.astype(F32), 0.0).astype(jnp.bfloat16))
                left = left - piece.astype(F32)
        for p in planes:
            hot = one_hot_rows(cells[...], first_row + p * width, width, lanes)
            outs[0][p] = spread(hot, columns[0])
            for level in range(STEPS):
                first = 1 + 3 * level
                outs[1 + level][p] = (
                    spread(hot, columns[first + 2]) + spread(hot, columns[first + 1])
                ) + spread(hot, columns[first])

    counts, seen0, seen1, seen2, seen3 = run(
        receive, "receive", [whole] * 5, (receivers, seen), cost=2_000_000
    )

    def step1(a0, b0, field, lap_s, newer_s, scale, rest, rest_next, src, pulse, *outs):
        model_ghosts, lap, accel, newer, lap_next, newest, pad = outs
        clear_pads(pad)
        model_ghosts[0] = a0[2]
        model_ghosts[1] = b0[2]
        for r, n in rows:
            low, high = ghosts(a0, b0, r, n)
            for p in planes:
                at = (p, slice(r, r + n))
                outside = reach(low, high, p, depth)
                curved = lap_s[at] + outside
                lap[at] = curved
                accel[at] = curved + rest[at]
                value = newer_s[at] + scale[at] * outside
                newer[at] = value
                pad[p, PAD + r : PAD + r + n] = value
        for p in planes:
            for r, n in rows:
                at = (p, slice(r, r + n))
                curved = own_laplace(pad, p, r, n)
                lap_next[at] = curved
                newest[at] = (
                    2.0 * newer[at]
                    - field[at]
                    + scale[at] * (curved + (rest_next[at] - echo[0] * lap[at]))
                    + pulse[1] * src[at]
                )

    model_ghosts, lap0, accel0, p1, lap1s, p2s = run(
        step1,
        "step1",
        [pair] + [whole] * 5,
        (*got_now, now, lap0s, p1s, scaled, rest0, rest1, source, wavelet),
        [padded],
        smem=(9,),
    )
    partner_ghosts = shot_swap(model_ghosts, 1)

    def outer_scale(mine, other, low, high):
        slab, count = lax.axis_index("slab"), lax.axis_size("slab")
        even = lax.rem(slab, 2) == 0
        first = lax.rem(lax.axis_index("shot"), 2) == 0
        for r, n in rows:
            at = slice(r, r + n)
            for j in range(2):
                have = first if j == 0 else jnp.logical_not(first)
                from_a = jnp.where(have, mine[0, at], other[0, at])
                from_b = jnp.where(have, mine[1, at], other[1, at])
                for side, ref, at_end in (
                    (jnp.where(even, from_b, from_a), low, slab == 0),
                    (jnp.where(even, from_a, from_b), high, slab == count - 1),
                ):
                    value = courant / (side * side)
                    ref[j, at] = jnp.where(at_end, jnp.zeros_like(value), value)

    scale_low, scale_high = run(
        outer_scale, "outer_scale", [pair] * 2, (model_ghosts, partner_ghosts)
    )

    def step2(a1, b1, field, lap_s, newer_s, scale, s_low, s_high, rest, lap_old, *outs):
        lap, accel, newer, a, b = outs
        for r, n in rows:
            low, high = ghosts(a1, b1, r, n)
            low, high = complete(low, high, s_low, s_high, field, r, n)
            for p in planes:
                at = (p, slice(r, r + n))
                outside = reach(low, high, p, depth)
                curved = lap_s[at] + outside
                lap[at] = curved
                accel[at] = curved + (rest[at] - echo[0] * lap_old[at])
                newer[at] = newer_s[at] + scale[at] * outside
        send_planes(a, b, newer)

    lap1, accel1, p2, *sends = run(
        step2,
        "step2",
        [whole] * 3 + [pair] * 2,
        (*got_p1, now, lap1s, p2s, scaled, scale_low, scale_high, rest1, lap0),
    )
    got_p2 = exchange(sends)

    def step3(field, before, scale, rest, lap_a, lap_b, src, pulse, *outs):
        accel_s, newer, a, b, pad = outs
        clear_pads(pad)
        for p in planes:
            pad[p, PAD : PAD + width] = field[p]
        for p in planes:
            for r, n in rows:
                at = (p, slice(r, r + n))
                part = rest[at] - echo[0] * lap_b[at] - echo[1] * lap_a[at]
                accel = own_laplace(pad, p, r, n) + part
                accel_s[at] = accel
                newer[at] = (
                    2.0 * field[at] - before[at] + scale[at] * accel + pulse[2] * src[at]
                )
        send_planes(a, b, newer)

    accel2s, p3s, *sends = run(
        step3,
        "step3",
        [whole] * 2 + [pair] * 2,
        (p2, p1, scaled, rest2, lap0, lap1, source, wavelet),
        [padded],
        smem=(7,),
    )
    got_p3 = exchange(sends)

    def step4(a2, b2, field, accel_s, newer_s, scale, rest2_, rest3_, lap_a, lap_b, src, pulse, *outs):
        accel, newer, accel_next, newest, pad = outs
        clear_pads(pad)
        for r, n in rows:
            low, high = ghosts(a2, b2, r, n)
            for p in planes:
                at = (p, slice(r, r + n))
                outside = reach(low, high, p, depth)
                accel[at] = accel_s[at] + outside
                value = newer_s[at] + scale[at] * outside
                newer[at] = value
                pad[p, PAD + r : PAD + r + n] = value
        for p in planes:
            for r, n in rows:
                at = (p, slice(r, r + n))
                lap_c = accel[at] - (rest2_[at] - echo[0] * lap_b[at] - echo[1] * lap_a[at])
                part = rest3_[at] - echo[0] * lap_c - echo[1] * lap_b[at] - echo[2] * lap_a[at]
                acc = own_laplace(pad, p, r, n) + part
                accel_next[at] = acc
                newest[at] = (
                    2.0 * newer[at] - field[at] + scale[at] * acc + pulse[3] * src[at]
                )

    accel2, p3, accel3s, p4s = run(
        step4,
        "step4",
        [whole] * 4,
        (*got_p2, p2, accel2s, p3s, scaled, rest2, rest3, lap0, lap1, source, wavelet),
        [padded],
        smem=(11,),
    )

    def turn(a3, b3, field, accel_s, newer_s, scale, s_low, s_high, hits, sums, back, *outs):
        united, drive, total, a, b = outs
        for r, n in rows:
            low, high = ghosts(a3, b3, r, n)
            low, high = complete(low, high, s_low, s_high, field, r, n)
            for p in planes:
                at = (p, slice(r, r + n))
                outside = reach(low, high, p, depth)
                newest = newer_s[at] + scale[at] * outside
                value = back[at] + (hits[at] * newest - sums[at])
                united[at] = value
                drive[at] = scale[at] * value
                total[at] = value * (accel_s[at] + outside)
        send_planes(a, b, drive)

    united3, drive3, accum, *sends = run(
        turn,
        "turn",
        [whole] * 3 + [pair] * 2,
        (*got_p3, p2, accel3s, p4s, scaled, scale_low, scale_high, counts, seen3, back_now),
    )
    got_d3 = exchange(sends)

    def adjoint3(field, drive, back, scale, hits, pressure, sums, *outs):
        united, drive_next, a, b, pad = outs
        clear_pads(pad)
        for p in planes:
            pad[p, PAD : PAD + width] = drive[p]
        for p in planes:
            for r, n in rows:
                at = (p, slice(r, r + n))
                value = (
                    back[at]
                    + 2.0 * field[at]
                    + own_laplace(pad, p, r, n)
                    + (hits[at] * pressure[at] - sums[at])
                )
                united[at] = value
                drive_next[at] = scale[at] * value - echo[0] * drive[at]
        send_planes(a, b, drive_next)

    united2s, drive2s, *sends = run(
        adjoint3,
        "adjoint3",
        [whole] * 2 + [pair] * 2,
        (united3, drive3, back_prev, scaled, counts, p3, seen2),
        [padded],
    )
    got_d2 = exchange(sends)

    def adjoint2(
        a4, b4, united_s, drive_s, scale, drive_old, united_old, hits, pressure, sums, accel, acc, *outs
    ):
        united, drive, total, united_next, drive_next, pad = outs
        clear_pads(pad)
        for r, n in rows:
            low, high = ghosts(a4, b4, r, n)
            for p in planes:
                at = (p, slice(r, r + n))
                outside = reach(low, high, p, depth)
                value = united_s[at] + outside
                united[at] = value
                total[at] = acc[at] + value * accel[at]
                pushed = drive_s[at] + scale[at] * outside
                drive[at] = pushed
                pad[p, PAD + r : PAD + r + n] = pushed
        for p in planes:
            for r, n in rows:
                at = (p, slice(r, r + n))
                value = (
                    2.0 * united[at]
                    - united_old[at]
                    + own_laplace(pad, p, r, n)
                    + (hits[at] * pressure[at] - sums[at])
                )
                united_next[at] = value
                drive_next[at] = (
                    scale[at] * (value - echo[0] * united[at]) - echo[1] * drive_old[at]
                )

    united2, drive2, accum, united1s, drive1s = run(
        adjoint2,
        "adjoint2",
        [whole] * 5,
        (
            *got_d3,
            united2s,
            drive2s,
            scaled,
            drive3,
            united3,
            counts,
            p2,
            seen1,
            accel2,
            accum,
        ),
        [padded],
    )

    def adjoint1(a5, b5, drive_old, united_s, drive_s, scale, s_low, s_high, *outs):
        united, drive, a, b = outs
        for r, n in rows:
            low, high = ghosts(a5, b5, r, n)
            low, high = complete(low, high, s_low, s_high, drive_old, r, n)
            for p in planes:
                at = (p, slice(r, r + n))
                outside = reach(low, high, p, depth)
                united[at] = united_s[at] + outside
                drive[at] = drive_s[at] + scale[at] * outside
        send_planes(a, b, drive)

    united1, drive1, *sends = run(
        adjoint1,
        "adjoint1",
        [whole] * 2 + [pair] * 2,
        (*got_d2, drive3, united1s, drive1s, scaled, scale_low, scale_high),
    )
    got_d1 = exchange(sends)

    def adjoint0(drive, united, united_old, hits, pressure, sums, accel_b, accel_a, acc, *outs):
        total, pad = outs
        clear_pads(pad)
        for p in planes:
            pad[p, PAD : PAD + width] = drive[p]
        for p in planes:
            for r, n in rows:
                at = (p, slice(r, r + n))
                value = (
                    2.0 * united[at]
                    - united_old[at]
                    + own_laplace(pad, p, r, n)
                    + (hits[at] * pressure[at] - sums[at])
                )
                total[at] = acc[at] + united[at] * accel_b[at] + value * accel_a[at]

    (accum,) = run(
        adjoint0,
        "adjoint0",
        [whole],
        (drive1, united1, united2, counts, p1, seen0, accel1, accel0, accum),
        [padded],
    )

    def finish(a6, b6, acc, accel, fact, keep, send, grad):
        mine = lax.rem(lax.axis_index("shot"), 2)
        for r, n in rows:
            low, high = ghosts(a6, b6, r, n)
            for p in planes:
                at = (p, slice(r, r + n))
                outside = reach(low, high, p, depth)
                grad[at] = fact[at] * (acc[at] + accel[at] * outside)
        for j in range(depth // 2):
            keep[j] = grad[mine * (depth // 2) + j]
            send[j] = grad[(1 - mine) * (depth // 2) + j]

    keep, give = run(
        finish,
        "finish",
        [half] * 2,
        (*got_d1, accum, accel0, factor),
        [pltpu.VMEM(whole, F32)],
    )

    def add(x, y, out):
        out[...] = x[...] + y[...]

    (part,) = run(add, "add", [half], (keep, shot_swap(give, 1)))
    bit = 2
    while bit < shots:
        (part,) = run(add, "add", [half], (part, shot_swap(part, bit)))
        bit *= 2

    def gather(mine_ref, other_ref, total, squares):
        mine = lax.rem(lax.axis_index("shot"), 2)
        acc = jnp.zeros((8, lanes), F32)
        for j in range(depth // 2):
            for ref, place in ((mine_ref, mine), (other_ref, 1 - mine)):
                value = ref[j]
                total[place * (depth // 2) + j] = value
                acc += jnp.sum((value * value).reshape(width // 8, 8, lanes), axis=0)
        squares[...] = acc

    total, squares = run(
        gather, "gather", [whole, (8, lanes)], (part, shot_swap(part, 1))
    )

    def add4(w, x, y, z, out):
        out[...] = (w[...] + x[...]) + (y[...] + z[...])

    bit = 1
    others = []
    while bit < slabs:
        if others:
            (squares,) = run(add4 if len(others) == 3 else add, "add_squares", [(8, lanes)], (squares, *others))
        if 2 * bit < slabs:
            others = [slab_swap(squares, k * bit) for k in (1, 2, 3)]
            bit *= 4
        else:
            others = [slab_swap(squares, bit)]
            bit *= 2

    share = width // shots
    cells_all = slabs * depth * width * lanes

    def update(field, model, *refs):
        sums, (new_model, gradient) = refs[:-2], refs[-2:]
        acc = sums[0][...]
        for ref in sums[1:]:
            acc = acc + ref[...]
        power = jnp.sum(acc, axis=(0, 1), keepdims=True)
        inverse = 1.0 / jnp.sqrt(power / cells_all + tiny_eps)
        first = pl.multiple_of(lax.axis_index("shot") * share, 8)
        for p in planes:
            for r, n in rows:
                at = (p, slice(r, r + n))
                new_model[at] = model[at] - update_rate * (field[at] * inverse)
            gradient[p] = field[p, pl.ds(first, share)] * inverse

    return run(
        update,
        "update",
        [whole, (depth, share, lanes)],
        (total, slowness, squares, *others),
    )


def solution(mesh):
    in_specs = (
        P(("groups", "slab"), None, None),
        P(("groups", "shot"), "slab", None, None),
        P(("groups", "shot"), "slab", None, None),
        P(("groups", "shot"), None, "slab", None, None),
        P(("groups", "shot"), "slab", None, None),
        P(("groups", "shot"), "slab", None, None),
        P(),
        P(("groups", "shot"), None),
        P(("groups", "shot"), None),
        P("groups"),
        P(("groups", "shot"), None, None),
    )
    out_specs = (P(("groups", "slab"), None, None), P(("groups", "slab"), "shot", None))
    return jax.shard_map(
        lambda *args: tuple(per_device(*args)),
        mesh=mesh,
        in_specs=in_specs,
        out_specs=out_specs,
        check_vma=False,
    )
```

```python
import jax
import jax.numpy as jnp
from jax import lax
from jax.experimental import pallas as pl
from jax.experimental.pallas import tpu as pltpu
from jax.sharding import PartitionSpec as P


STEPS = 4

center_coef = -2.5
near_coef = 4.0 / 3.0
far_coef = -1.0 / 12.0
courant = 0.14
relax_decay = (0.3, 0.7, 0.95)
relax_weight = (0.3, 0.2, 0.1)
update_rate = 0.05
tiny_eps = 1e-06

echo = tuple(
    sum(b * a**k for a, b in zip(relax_decay, relax_weight)) for k in range(STEPS)
)

PAD = 8
VMEM_SPEC = pl.BlockSpec(memory_space=pltpu.VMEM)
SMEM_SPEC = pl.BlockSpec(memory_space=pltpu.SMEM)
HBM_SPEC = pl.BlockSpec(memory_space=pltpu.HBM)
F32 = jnp.float32


def run(kernel, outs, args, scratch=(), hbm=(), cost=200_000):
    specs = [HBM_SPEC if i in hbm else VMEM_SPEC for i in range(len(args))]
    args = [
        pltpu.with_memory_space_constraint(arg, pltpu.HBM) if i in hbm else arg
        for i, arg in enumerate(args)
    ]
    return pl.pallas_call(
        kernel,
        out_shape=[jax.ShapeDtypeStruct(shape, F32) for shape in outs],
        in_specs=specs,
        out_specs=[VMEM_SPEC] * len(outs),
        scratch_shapes=list(scratch),
        compiler_params=pltpu.CompilerParams(vmem_limit_bytes=12 << 20),
        cost_estimate=pl.CostEstimate(flops=cost, bytes_accessed=cost, transcendentals=0),
    )(*args)


def chunks(width):
    step = 64 if width % 64 == 0 else 8
    return [(start, step) for start in range(0, width, step)]


def clear_pads(pad):
    depth, tall, lanes = pad.shape
    for p in range(depth):
        pad[p, :PAD] = jnp.zeros((PAD, lanes), F32)
        pad[p, tall - PAD :] = jnp.zeros((PAD, lanes), F32)


def own_laplace(pad, p, r, n):
    depth, _, lanes = pad.shape

    def at(plane, shift):
        return pad[plane, PAD + r + shift : PAD + r + shift + n]

    middle = at(p, 0)
    near = at(p, 1) + at(p, -1)
    far = at(p, 2) + at(p, -2)
    for plane in (p - 1, p + 1):
        if 0 <= plane < depth:
            near += at(plane, 0)
    for plane in (p - 2, p + 2):
        if 0 <= plane < depth:
            far += at(plane, 0)
    lane = lax.broadcasted_iota(jnp.int32, (n, lanes), 1)
    near += jnp.where(lane >= 1, pltpu.roll(middle, 1, 1), 0.0)
    near += jnp.where(lane < lanes - 1, pltpu.roll(middle, lanes - 1, 1), 0.0)
    far += jnp.where(lane >= 2, pltpu.roll(middle, 2, 1), 0.0)
    far += jnp.where(lane < lanes - 2, pltpu.roll(middle, lanes - 2, 1), 0.0)
    return 3.0 * center_coef * middle + near_coef * near + far_coef * far


def ghosts(a, b, r, n):
    slab, count = lax.axis_index("slab"), lax.axis_size("slab")
    even = lax.rem(slab, 2) == 0
    low, high = [], []
    for j in range(2):
        from_a, from_b = a[j, r : r + n], b[j, r : r + n]
        zero = jnp.zeros_like(from_a)
        low.append(jnp.where(slab == 0, zero, jnp.where(even, from_b, from_a)))
        high.append(jnp.where(slab == count - 1, zero, jnp.where(even, from_a, from_b)))
    return low, high


def reach(low, high, p, depth):
    terms = []
    for distance, coef in ((1, near_coef), (2, far_coef)):
        below, above = p - distance, p + distance
        if below < 0:
            terms.append(coef * low[2 + below])
        if above >= depth:
            terms.append(coef * high[above - depth])
    return sum(terms[1:], terms[0]) if terms else 0.0


def complete(low, high, scale_low, scale_high, field, r, n):
    depth = field.shape[0]

    def row(p):
        return field[p, r : r + n]

    low = [
        low[0] + scale_low[0, r : r + n] * (far_coef * row(0)),
        low[1] + scale_low[1, r : r + n] * (near_coef * row(0) + far_coef * row(1)),
    ]
    high = [
        high[0]
        + scale_high[0, r : r + n] * (near_coef * row(depth - 1) + far_coef * row(depth - 2)),
        high[1] + scale_high[1, r : r + n] * (far_coef * row(depth - 1)),
    ]
    return low, high


def send_planes(a, b, field):
    depth = field.shape[0]
    odd = lax.rem(lax.axis_index("slab"), 2)
    top = depth - 2
    for j in range(2):
        a[j] = field[top * (1 - odd) + j]
        b[j] = field[top * odd + j]


def one_hot_rows(cells, first_row, rows, lanes):
    shift = lanes.bit_length() - 1
    row = lax.shift_right_arithmetic(cells, shift) - first_row
    at = lax.broadcasted_iota(jnp.int32, (rows, cells.shape[1]), 0)
    return jnp.where(at == row, 1.0, 0.0).astype(jnp.bfloat16)


def is_lane(cells, lanes):
    at = lax.broadcasted_iota(jnp.int32, (lanes, cells.shape[1]), 0)
    return at == jnp.bitwise_and(cells, lanes - 1)


def spread(rows, columns):
    return lax.dot_general(
        rows, columns, (((1,), (1,)), ((), ())), preferred_element_type=F32
    )


def per_device(
    slowness,
    wave_prev,
    wave_now,
    memory,
    adjoint_now,
    adjoint_prev,
    wavelet,
    src_cells,
    src_signs,
    rec_cells,
    observed,
):
    depth, width, lanes = slowness.shape
    slabs, shots = lax.axis_size("slab"), lax.axis_size("shot")
    mechanisms = memory.shape[1]
    assert depth >= 4 and depth % 2 == 0 and lanes & (lanes - 1) == 0
    assert slabs & (slabs - 1) == 0 and shots & (shots - 1) == 0 and shots > 1 and slabs > 1
    whole, pair, half = (depth, width, lanes), (2, width, lanes), (depth // 2, width, lanes)
    rows = chunks(width)
    planes = range(depth)
    padded = pltpu.VMEM((depth, width + 2 * PAD, lanes), F32)
    older, now, relax = wave_prev[0], wave_now[0], memory[0]
    back_now, back_prev = adjoint_now[0], adjoint_prev[0]
    receivers = rec_cells.reshape(1, -1)
    seen = observed[0]

    pairs_a = [(i, i ^ 1) for i in range(slabs)]
    pairs_b = []
    for s in range(shots):
        for k in range(slabs):
            mate = k + 1 if k % 2 else k - 1
            if 0 <= mate < slabs:
                pairs_b.append((s * slabs + k, s * slabs + mate))
            else:
                pairs_b.append((s * slabs + k, (s ^ 1) * slabs + k))

    def exchange(sends):
        got_a = lax.ppermute(sends[0], "slab", pairs_a)
        got_b = lax.ppermute(sends[1], ("shot", "slab"), pairs_b)
        return got_a, got_b

    def shot_swap(value, bit):
        return lax.ppermute(value, "shot", [(i, i ^ bit) for i in range(shots)])

    def slab_swap(value, bit):
        return lax.ppermute(value, "slab", [(i, i ^ bit) for i in range(slabs)])

    def first_sends(field, model, a, b, arrived):
        odd = lax.rem(lax.axis_index("slab"), 2)
        mine = lax.rem(lax.axis_index("shot"), 2)
        top = depth - 2
        copies = []
        for k, (out, first) in enumerate(((a, top * (1 - odd)), (b, top * odd))):
            copies.append(
                pltpu.make_async_copy(field.at[pl.ds(first, 2)], out.at[0:2], arrived.at[2 * k])
            )
            copies.append(
                pltpu.make_async_copy(model.at[first + mine], out.at[2], arrived.at[2 * k + 1])
            )
        for copy in copies:
            copy.start()
        for copy in copies:
            copy.wait()

    got0 = exchange(
        run(
            first_sends,
            [(3, width, lanes)] * 2,
            (now, slowness),
            [pltpu.SemaphoreType.DMA((4,))],
            hbm=(0, 1),
        ),
    )

    def step0(*refs):
        sources, refs = refs[:7], refs[7:]
        field, model, lap, newer, scaled, factor = refs[:6]
        pushes, rests, (a, b), refs = refs[6:9], refs[9:13], refs[13:15], refs[15:]
        before, variables, cells, signs, pulse, source, pad, arrived = refs
        targets = (field, cells, signs, pulse, model, variables, before)
        copies = [
            pltpu.make_async_copy(src, dst, arrived.at[i])
            for i, (src, dst) in enumerate(zip(sources, targets))
        ]
        for copy in copies:
            copy.start()
        clear_pads(pad)
        first_row = lax.axis_index("slab") * (depth * width)
        for copy in copies[:4]:
            copy.wait()
        columns = jnp.where(is_lane(cells[...], lanes), signs[...].astype(F32), 0.0)
        columns = columns.astype(jnp.bfloat16)
        for p in planes:
            source[p] = spread(
                one_hot_rows(cells[...], first_row + p * width, width, lanes), columns
            )
            pad[p, PAD : PAD + width] = field[p]
        for copy in copies[4:]:
            copy.wait()
        for p in planes:
            for r, n in rows:
                at = (p, slice(r, r + n))
                inverse = 1.0 / model[at]
                scale = courant * (inverse * inverse)
                scaled[at] = scale
                factor[at] = -2.0 * (scale * inverse)
                parts = [variables[(l, *at)] for l in range(mechanisms)]
                for n_step in range(STEPS):
                    terms = [
                        part if n_step == 0 else a_l**n_step * part
                        for part, a_l in zip(parts, relax_decay)
                    ]
                    rests[n_step][at] = sum(terms[1:], terms[0])
                curved = own_laplace(pad, p, r, n)
                lap[at] = curved
                shape = source[at]
                newer[at] = (
                    2.0 * field[at]
                    - before[at]
                    + scale * (curved + rests[0][at])
                    + pulse[0] * shape
                )
                for n_step in range(1, STEPS):
                    pushes[n_step - 1][at] = pulse[n_step] * shape
        send_planes(a, b, newer)

    now, model, lap0s, p1s, scaled, factor, *fields = run(
        step0,
        [whole] * 13 + [pair] * 2,
        (now, src_cells, src_signs, wavelet, slowness, relax, older),
        [
            pltpu.VMEM(whole, F32),
            pltpu.VMEM(relax.shape, F32),
            pltpu.VMEM(src_cells.shape, jnp.int32),
            pltpu.VMEM(src_signs.shape, jnp.int32),
            pltpu.SMEM(wavelet.shape, F32),
            pltpu.VMEM(whole, F32),
            padded,
            pltpu.SemaphoreType.DMA((7,)),
        ],
        hbm=range(7),
    )
    (push1, push2, push3), (rest0, rest1, rest2, rest3), sends = fields[:3], fields[3:7], fields[7:]
    got1 = exchange(sends)

    def receive(cells, values, *outs):
        first_row = lax.axis_index("slab") * (depth * width)
        lane = is_lane(cells[...], lanes)
        columns = [jnp.where(lane, 1.0, 0.0).astype(jnp.bfloat16)]
        for level in range(STEPS):
            left = values[level : level + 1, :]
            for _ in range(3):
                piece = left.astype(jnp.bfloat16)
                columns.append(jnp.where(lane, piece.astype(F32), 0.0).astype(jnp.bfloat16))
                left = left - piece.astype(F32)
        for p in planes:
            hot = one_hot_rows(cells[...], first_row + p * width, width, lanes)
            outs[0][p] = spread(hot, columns[0])
            for level in range(STEPS):
                first = 1 + 3 * level
                outs[3 + level][p] = (
                    spread(hot, columns[first + 2]) + spread(hot, columns[first + 1])
                ) + spread(hot, columns[first])
        for j in range(2):
            for out, p in ((outs[1], j - 2), (outs[2], depth + j)):
                hot = one_hot_rows(cells[...], first_row + p * width, width, lanes)
                out[j] = spread(hot, columns[0])

    counts, counts_low, counts_high, seen0, seen1, seen2, seen3 = run(
        receive, [whole] + [pair] * 2 + [whole] * STEPS, (receivers, seen), cost=2_000_000
    )

    def forward1(a, b, field, lap_s, newer_s, scale, rest, rest_next, push, ready, *outs):
        del ready
        model_ghosts, lap, accel, newer, lap_next, newest, out_a, out_b, pad = outs
        clear_pads(pad)
        model_ghosts[0] = a[2]
        model_ghosts[1] = b[2]
        for r, n in rows:
            low, high = ghosts(a, b, r, n)
            for p in planes:
                at = (p, slice(r, r + n))
                outside = reach(low, high, p, depth)
                curved = lap_s[at] + outside
                lap[at] = curved
                accel[at] = curved + rest[at]
                value = newer_s[at] + scale[at] * outside
                newer[at] = value
                pad[p, PAD + r : PAD + r + n] = value
        for p in planes:
            for r, n in rows:
                at = (p, slice(r, r + n))
                curved = own_laplace(pad, p, r, n)
                lap_next[at] = curved
                newest[at] = (
                    2.0 * newer[at]
                    - field[at]
                    + scale[at] * (curved + (rest_next[at] - echo[0] * lap[at]))
                    + push[at]
                )
        send_planes(out_a, out_b, newest)

    model_ghosts, lap0, accel0, p1, lap1s, p2s, *sends = run(
        forward1,
        [pair] + [whole] * 5 + [pair] * 2,
        (*got0, now, lap0s, p1s, scaled, rest0, rest1, push1, counts_low),
        [padded],
    )
    got2 = exchange(sends)
    partner_ghosts = shot_swap(model_ghosts, 1)

    def outer_scale(mine, other, hits_low, hits_high, low, high, turn_low, turn_high):
        slab, count = lax.axis_index("slab"), lax.axis_size("slab")
        even = lax.rem(slab, 2) == 0
        first = lax.rem(lax.axis_index("shot"), 2) == 0
        for r, n in rows:
            at = slice(r, r + n)
            for j in range(2):
                have = first if j == 0 else jnp.logical_not(first)
                from_a = jnp.where(have, mine[0, at], other[0, at])
                from_b = jnp.where(have, mine[1, at], other[1, at])
                for side, ref, turn, hits, at_end in (
                    (jnp.where(even, from_b, from_a), low, turn_low, hits_low, slab == 0),
                    (jnp.where(even, from_a, from_b), high, turn_high, hits_high, slab == count - 1),
                ):
                    value = courant / (side * side)
                    value = jnp.where(at_end, jnp.zeros_like(value), value)
                    ref[j, at] = value
                    turn[j, at] = value * value * hits[j, at]

    scale_low, scale_high, turn_low, turn_high = run(
        outer_scale, [pair] * 4, (model_ghosts, partner_ghosts, counts_low, counts_high)
    )

    def forward2(
        a, b, older_, s_low, s_high, lap_s, newer_s, scale, rest, lap_old, field, rest_next, push, *outs
    ):
        lap, accel, newer, accel_s, newest, out_a, out_b, pad = outs
        clear_pads(pad)
        for r, n in rows:
            low, high = ghosts(a, b, r, n)
            low, high = complete(low, high, s_low, s_high, older_, r, n)
            for p in planes:
                at = (p, slice(r, r + n))
                outside = reach(low, high, p, depth)
                curved = lap_s[at] + outside
                lap[at] = curved
                accel[at] = curved + (rest[at] - echo[0] * lap_old[at])
                value = newer_s[at] + scale[at] * outside
                newer[at] = value
                pad[p, PAD + r : PAD + r + n] = value
        for p in planes:
            for r, n in rows:
                at = (p, slice(r, r + n))
                part = rest_next[at] - echo[0] * lap[at] - echo[1] * lap_old[at]
                acc = own_laplace(pad, p, r, n) + part
                accel_s[at] = acc
                newest[at] = 2.0 * newer[at] - field[at] + scale[at] * acc + push[at]
        send_planes(out_a, out_b, newest)

    lap1, accel1, p2, accel2s, p3s, *sends = run(
        forward2,
        [whole] * 5 + [pair] * 2,
        (
            *got1,
            now,
            scale_low,
            scale_high,
            lap1s,
            p2s,
            scaled,
            rest1,
            lap0,
            p1,
            rest2,
            push2,
        ),
        [padded],
    )
    got3 = exchange(sends)

    def forward3(
        a,
        b,
        older_,
        s_low,
        s_high,
        accel_old,
        newer_s,
        scale,
        rest2_,
        rest3_,
        lap_a,
        lap_b,
        field,
        push,
        hits,
        sums,
        back,
        *outs,
    ):
        accel, newer, accel_s, united_s, drive_s, out_a, out_b, pad = outs
        clear_pads(pad)
        for r, n in rows:
            low, high = ghosts(a, b, r, n)
            low, high = complete(low, high, s_low, s_high, older_, r, n)
            for p in planes:
                at = (p, slice(r, r + n))
                outside = reach(low, high, p, depth)
                accel[at] = accel_old[at] + outside
                value = newer_s[at] + scale[at] * outside
                newer[at] = value
                pad[p, PAD + r : PAD + r + n] = value
        for p in planes:
            for r, n in rows:
                at = (p, slice(r, r + n))
                lap_c = accel[at] - (rest2_[at] - echo[0] * lap_b[at] - echo[1] * lap_a[at])
                part = rest3_[at] - echo[0] * lap_c - echo[1] * lap_b[at] - echo[2] * lap_a[at]
                acc = own_laplace(pad, p, r, n) + part
                accel_s[at] = acc
                newest = 2.0 * newer[at] - field[at] + scale[at] * acc + push[at]
                value = back[at] + (hits[at] * newest - sums[at])
                united_s[at] = value
                drive_s[at] = scale[at] * value
        send_planes(out_a, out_b, drive_s)

    accel2, p3, accel3s, united3s, drive3s, *sends = run(
        forward3,
        [whole] * 5 + [pair] * 2,
        (
            *got2,
            p1,
            scale_low,
            scale_high,
            accel2s,
            p3s,
            scaled,
            rest2,
            rest3,
            lap0,
            lap1,
            p2,
            push3,
            counts,
            seen3,
            back_now,
        ),
        [padded],
    )
    got4 = exchange(sends)

    def forward4(
        a,
        b,
        older_,
        s_low,
        s_high,
        accel_old,
        united_old,
        drive_old,
        scale,
        hits,
        back,
        pressure,
        sums,
        *outs,
    ):
        united, drive, total, united_s, drive_s, out_a, out_b, pad = outs
        clear_pads(pad)
        for r, n in rows:
            low, high = ghosts(a, b, r, n)
            low, high = complete(low, high, s_low, s_high, older_, r, n)
            for p in planes:
                at = (p, slice(r, r + n))
                outside = reach(low, high, p, depth)
                change = hits[at] * (scale[at] * outside)
                value = united_old[at] + change
                united[at] = value
                total[at] = value * (accel_old[at] + outside)
                pushed = drive_old[at] + scale[at] * change
                drive[at] = pushed
                pad[p, PAD + r : PAD + r + n] = pushed
        for p in planes:
            for r, n in rows:
                at = (p, slice(r, r + n))
                value = (
                    back[at]
                    + 2.0 * united[at]
                    + own_laplace(pad, p, r, n)
                    + (hits[at] * pressure[at] - sums[at])
                )
                united_s[at] = value
                drive_s[at] = scale[at] * value - echo[0] * drive[at]
        send_planes(out_a, out_b, drive_s)

    united3, drive3, accum, united2s, drive2s, *sends = run(
        forward4,
        [whole] * 5 + [pair] * 2,
        (
            *got3,
            p2,
            scale_low,
            scale_high,
            accel3s,
            united3s,
            drive3s,
            scaled,
            counts,
            back_prev,
            p3,
            seen2,
        ),
        [padded],
    )
    got5 = exchange(sends)

    def adjoint2(
        a,
        b,
        older_,
        s_low,
        s_high,
        united_s,
        drive_s,
        scale,
        drive_old,
        united_old,
        hits,
        pressure,
        sums,
        accel,
        acc,
        *outs,
    ):
        united, drive, total, united_next, drive_next, out_a, out_b, pad = outs
        clear_pads(pad)
        for r, n in rows:
            low, high = ghosts(a, b, r, n)
            low, high = complete(low, high, s_low, s_high, older_, r, n)
            for p in planes:
                at = (p, slice(r, r + n))
                outside = reach(low, high, p, depth)
                value = united_s[at] + outside
                united[at] = value
                total[at] = acc[at] + value * accel[at]
                pushed = drive_s[at] + scale[at] * outside
                drive[at] = pushed
                pad[p, PAD + r : PAD + r + n] = pushed
        for p in planes:
            for r, n in rows:
                at = (p, slice(r, r + n))
                value = (
                    2.0 * united[at]
                    - united_old[at]
                    + own_laplace(pad, p, r, n)
                    + (hits[at] * pressure[at] - sums[at])
                )
                united_next[at] = value
                drive_next[at] = (
                    scale[at] * (value - echo[0] * united[at]) - echo[1] * drive_old[at]
                )
        send_planes(out_a, out_b, drive_next)

    united2, drive2, accum, united1s, drive1s, *sends = run(
        adjoint2,
        [whole] * 5 + [pair] * 2,
        (
            *got4,
            p3,
            turn_low,
            turn_high,
            united2s,
            drive2s,
            scaled,
            drive3,
            united3,
            counts,
            p2,
            seen1,
            accel2,
            accum,
        ),
        [padded],
    )
    got6 = exchange(sends)

    def adjoint1(
        a,
        b,
        older_,
        s_low,
        s_high,
        united_s,
        drive_s,
        scale,
        united_old,
        hits,
        pressure,
        sums,
        accel_b,
        accel_a,
        acc,
        total,
        united,
        pad,
    ):
        clear_pads(pad)
        for r, n in rows:
            low, high = ghosts(a, b, r, n)
            low, high = complete(low, high, s_low, s_high, older_, r, n)
            for p in planes:
                at = (p, slice(r, r + n))
                outside = reach(low, high, p, depth)
                united[at] = united_s[at] + outside
                pad[p, PAD + r : PAD + r + n] = drive_s[at] + scale[at] * outside
        for p in planes:
            for r, n in rows:
                at = (p, slice(r, r + n))
                value = (
                    2.0 * united[at]
                    - united_old[at]
                    + own_laplace(pad, p, r, n)
                    + (hits[at] * pressure[at] - sums[at])
                )
                total[at] = acc[at] + united[at] * accel_b[at] + value * accel_a[at]

    (accum,) = run(
        adjoint1,
        [whole],
        (
            *got5,
            drive3,
            scale_low,
            scale_high,
            united1s,
            drive1s,
            scaled,
            united2,
            counts,
            p1,
            seen0,
            accel1,
            accel0,
            accum,
        ),
        [pltpu.VMEM(whole, F32), padded],
    )

    def finish(a, b, older_, s_low, s_high, acc, accel, fact, keep, send, grad):
        mine = lax.rem(lax.axis_index("shot"), 2)
        for r, n in rows:
            low, high = ghosts(a, b, r, n)
            low, high = complete(low, high, s_low, s_high, older_, r, n)
            for p in planes:
                at = (p, slice(r, r + n))
                outside = reach(low, high, p, depth)
                grad[at] = fact[at] * (acc[at] + accel[at] * outside)
        for j in range(depth // 2):
            keep[j] = grad[mine * (depth // 2) + j]
            send[j] = grad[(1 - mine) * (depth // 2) + j]

    keep, give = run(
        finish,
        [half] * 2,
        (*got6, drive2, scale_low, scale_high, accum, accel0, factor),
        [pltpu.VMEM(whole, F32)],
    )

    def add(x, y, out):
        out[...] = x[...] + y[...]

    (part,) = run(add, [half], (keep, shot_swap(give, 1)))
    bit = 2
    while bit < shots:
        (part,) = run(add, [half], (part, shot_swap(part, bit)))
        bit *= 2

    def gather(mine_ref, other_ref, total, squares):
        mine = lax.rem(lax.axis_index("shot"), 2)
        acc = jnp.zeros((8, lanes), F32)
        for j in range(depth // 2):
            for ref, place in ((mine_ref, mine), (other_ref, 1 - mine)):
                value = ref[j]
                total[place * (depth // 2) + j] = value
                acc += jnp.sum((value * value).reshape(width // 8, 8, lanes), axis=0)
        squares[...] = acc

    total, squares = run(gather, [whole, (8, lanes)], (part, shot_swap(part, 1)))

    def add4(w, x, y, z, out):
        out[...] = (w[...] + x[...]) + (y[...] + z[...])

    bit = 1
    others = []
    while bit < slabs:
        if others:
            (squares,) = run(add4 if len(others) == 3 else add, [(8, lanes)], (squares, *others))
        if 2 * bit < slabs:
            others = [slab_swap(squares, k * bit) for k in (1, 2, 3)]
            bit *= 4
        else:
            others = [slab_swap(squares, bit)]
            bit *= 2

    share = width // shots
    cells_all = slabs * depth * width * lanes

    def update(field, model, *refs):
        sums, (new_model, gradient) = refs[:-2], refs[-2:]
        acc = sums[0][...]
        for ref in sums[1:]:
            acc = acc + ref[...]
        power = jnp.sum(acc, axis=(0, 1), keepdims=True)
        inverse = 1.0 / jnp.sqrt(power / cells_all + tiny_eps)
        first = pl.multiple_of(lax.axis_index("shot") * share, 8)
        for p in planes:
            for r, n in rows:
                at = (p, slice(r, r + n))
                new_model[at] = model[at] - update_rate * (field[at] * inverse)
            gradient[p] = field[p, pl.ds(first, share)] * inverse

    return run(update, [whole, (depth, share, lanes)], (total, model, squares, *others))


def solution(mesh):
    in_specs = (
        P(("groups", "slab"), None, None),
        P(("groups", "shot"), "slab", None, None),
        P(("groups", "shot"), "slab", None, None),
        P(("groups", "shot"), None, "slab", None, None),
        P(("groups", "shot"), "slab", None, None),
        P(("groups", "shot"), "slab", None, None),
        P(),
        P(("groups", "shot"), None),
        P(("groups", "shot"), None),
        P("groups"),
        P(("groups", "shot"), None, None),
    )
    out_specs = (P(("groups", "slab"), None, None), P(("groups", "slab"), "shot", None))

    def body(*args):
        return tuple(per_device(*args))

    return jax.shard_map(
        body, mesh=mesh, in_specs=in_specs, out_specs=out_specs, check_vma=False
    )
```
